256 devices in a mesh: alpha: 16 (over y_hi, x, core), beta: 16 (over y_lo, z).
Axes of the slice: x: 4, y: 4 (y_hi: 2, y_lo: 2; y = y_hi * 2 + y_lo), z: 8, core: 2. Of those that a mesh axis runs over, the one named last changes fastest.
Arguments:
- coefficients: bfloat16 [8192, 16384], P('alpha', 'beta'), may hold values from -6 to 6
- couplings: bfloat16 [8, 256, 256], replicated, may hold values from -0.375 to 0.375
- exc_list: int32 [16, 16, 3], replicated, may hold values from 0 to 31, as said below
- counts: int32 [16, 16], replicated, may hold values from 0 to 1, as said below
- beta_tiles: bfloat16 [4, 1024, 16384], P(None, None, 'beta'), may hold values from -0.09375 to 0.09375
Outputs:
- sigma_vector: float32 [8192, 16384], P('alpha', 'beta')
The draws below stay inside these ranges and needn't reach their ends.
Inputs may be any that keep to these rules, and one draw needn't show every extreme that they name: `exc_list`: entry [s, p] describes the slot from alpha device s to alpha device p: field 0 is a source block held by device s (from s * 2 to s * 2 + 1), field 1 a target block held by device p (from p * 2 to p * 2 + 1), field 2 a coupling index below 8. `counts`: 1 where a slot is live, 0 where it is empty; in every draw some device p has a live slot from every device s.
All inputs are finite; a program needn't handle non-finite values.
Results may differ from the reference program's by a relative error of at most 0.0029.
Values may be sent and summed in bfloat16 or wider, within the bound.
No kernel may reach another device: no remote copies, remote signals or barrier semaphores. Data moves between devices by JAX's collectives and lax.ppermute only.
A program may use at most 192 MiB of HBM per device.

```python
import jax
import jax.numpy as jnp
from jax import lax

AB = 256
BB = 1024
ABLK = 2
KC = 8
STOPS = 4
NA = 8192
NBETA = 16384
N_ALPHA = 16
N_BETA = 16


def route_tables(key):
    key = jax.random.fold_in(key, 7)
    key_dest, key_live, key_source, key_target, key_kind = jax.random.split(key, 5)
    full_dest = jax.random.randint(key_dest, (), 0, N_ALPHA)
    device_range = jnp.arange(N_ALPHA, dtype=jnp.int32)
    is_live = jax.random.randint(key_live, (N_ALPHA, N_ALPHA), 0, 5) < 2
    is_live = is_live | (device_range[None, :] == full_dest)
    occupancy = is_live.astype(jnp.int32)
    source = device_range[:, None] * ABLK + jax.random.randint(key_source, (N_ALPHA, N_ALPHA), 0, ABLK)
    target = device_range[None, :] * ABLK + jax.random.randint(key_target, (N_ALPHA, N_ALPHA), 0, ABLK)
    coupling_index = jax.random.randint(key_kind, (N_ALPHA, N_ALPHA), 0, KC)
    entries = jnp.stack([source, target, coupling_index], axis=-1).astype(jnp.int32)
    return (entries, occupancy)


def draw_exc_list(key, part):
    return route_tables(key)[0]


def draw_counts(key, part):
    return route_tables(key)[1]


def steps_of(key, extent, pieces, low, largest):
    def one(dim, blocks):
        draws = jax.random.uniform(jax.random.fold_in(jax.random.fold_in(key, 6), dim), (blocks,), jnp.float32, low / len(pieces), largest / len(pieces))
        return jnp.repeat(jnp.exp(draws), extent[dim] // blocks).reshape((-1,) + (1,) * (len(extent) - dim - 1))

    level = one(*pieces[0])
    for cut in pieces[1:]:
        level = level * one(*cut)
    return level


def noise(rng, shape, deviation, bound, cuts=(), kind=jnp.bfloat16):
    result = jax.random.normal(rng, shape, jnp.float32) * deviation
    if len(cuts) > 0:
        result = steps_of(rng, shape, cuts, -0.22, 0.18) * result
    return jnp.clip(result, min=-bound, max=bound).astype(kind)


def setup_inputs(seed: int = 0) -> dict:
    key_of = jax.random.split(jax.random.key(seed), 6)
    coefficients = noise(key_of[0], (NA, NBETA), 1.0, 6.0, ((0, 16), (1, 16)))
    couplings = noise(key_of[1], (KC, AB, AB), AB ** -0.5, 0.375)
    exc_list = draw_exc_list(jax.random.fold_in(key_of[5], 71), 0)
    counts = draw_counts(jax.random.fold_in(key_of[5], 71), 0)
    beta_tiles = noise(key_of[4], (STOPS, BB, NBETA), (STOPS * BB) ** -0.5, 0.09375, ((2, 16),))
    return dict(coefficients=coefficients, couplings=couplings, exc_list=exc_list, counts=counts, beta_tiles=beta_tiles)


def reference(coefficients, couplings, exc_list, counts, beta_tiles):
    block_count = ABLK * N_ALPHA
    blocks = coefficients.astype(jnp.float32).reshape(block_count, AB * NBETA)
    weights_cat = jnp.transpose(couplings.astype(jnp.float32), (1, 0, 2)).reshape(AB, KC * AB)
    coupling_range = jnp.arange(KC, dtype=jnp.int32)
    block_range = jnp.arange(block_count, dtype=jnp.int32)

    def one_target(target):
        owner_device = target // ABLK
        is_live = (counts[:, owner_device] == 1) & (exc_list[:, owner_device, 1] == target)
        source = exc_list[:, owner_device, 0]
        coupling_index = exc_list[:, owner_device, 2]
        onehot = ((coupling_index[None, :] == coupling_range[:, None]) & is_live[None, :]).astype(jnp.float32)
        source_hot = (source[:, None] == block_range[None, :]).astype(jnp.float32)
        grouping = jnp.dot(onehot, source_hot, precision=lax.Precision.HIGHEST)
        grouped = jnp.dot(grouping, blocks, precision=lax.Precision.HIGHEST).reshape(KC * AB, NBETA)
        return jnp.dot(weights_cat, grouped, precision=lax.Precision.HIGHEST).astype(jnp.bfloat16)

    interm = lax.map(one_target, jnp.arange(block_count, dtype=jnp.int32)).reshape(block_count * AB, NBETA)

    def one_column(column):
        summed = jnp.zeros((block_count * AB, BB), jnp.float32)
        for offset in range(STOPS):
            anchor = (column - offset) % N_BETA
            shifted = lax.dynamic_slice_in_dim(interm, (anchor * BB).astype(jnp.int32), BB, 1).astype(jnp.float32)
            tile_block = lax.dynamic_slice_in_dim(beta_tiles[offset], (column * BB).astype(jnp.int32), BB, 1).astype(jnp.float32)
            summed = summed + jnp.dot(shifted, tile_block, precision=lax.Precision.HIGHEST)
        return summed

    results = lax.map(one_column, jnp.arange(N_BETA, dtype=jnp.int32))
    return jnp.transpose(results, (1, 0, 2)).reshape(block_count * AB, N_BETA * BB)
```

```python
import functools

import jax
import jax.numpy as jnp
from jax import lax
from jax.experimental import pallas as pl
from jax.experimental.pallas import tpu as pltpu
from jax.sharding import PartitionSpec as P

AB = 256
ABLK = 2
STOPS = 4
NX = 4
KC = 8
CHUNKS = (128, 256, 256, 384)


def device_of(y, x, core):
    return (y * NX + x) * 2 + core


def alpha_route(move):
    route = []
    for y in range(2):
        for x in range(NX):
            for core in range(2):
                to = move(y, x, core)
                route.append((device_of(y, x, core), device_of(*to)))
    return route


def to_x(step):
    return alpha_route(lambda y, x, core: (y, (x + step) % NX, core))


SWAP_CORE = alpha_route(lambda y, x, core: (y, x, 1 - core))
SWAP_Y = alpha_route(lambda y, x, core: (1 - y, x, core))


def next_beta(block):
    n = lax.axis_size("beta")
    return lax.ppermute(block, "beta", [(i, (i + 1) % n) for i in range(n)])


def couple_kernel(exc, counts, coup, own, left, right, far_a, far_b, sib, own_out, far_out, acc):
    me = lax.axis_index("alpha")
    y, x, core = me // (2 * NX), (me // 2) % NX, me % 2
    for which in range(2):
        side = y if which == 0 else 1 - y
        target_dev = device_of(side, x, core)
        acc[...] = jnp.zeros_like(acc)

        def slot(source_dev, take):
            live = counts[source_dev, target_dev] == 1
            src = jnp.clip(exc[source_dev, target_dev * 3] - source_dev * ABLK, 0, ABLK - 1)
            tgt = jnp.clip(exc[source_dev, target_dev * 3 + 1] - target_dev * ABLK, 0, ABLK - 1)
            kind = jnp.clip(exc[source_dev, target_dev * 3 + 2], 0, KC - 1)

            @pl.when(live)
            def _():
                rows = pl.ds(pl.multiple_of(tgt * AB, AB), AB)
                acc[rows, :] += jnp.dot(coup[kind], take(src), preferred_element_type=jnp.float32)

        def rows_of(ref, base):
            return lambda src: ref[pl.ds(pl.multiple_of(base + src * AB, AB), AB), :]

        for other in range(2):
            c = core if other == 0 else 1 - core
            for step in range(NX):
                source_dev = device_of(y, (x + step) % NX, c)
                if other == 0:
                    if step == 2:
                        take = lambda src: jnp.where(src == 0, far_a[...], far_b[...])
                    else:
                        take = rows_of({0: own, 1: right, 3: left}[step], 0)
                else:
                    take = rows_of(sib, step * ABLK * AB)
                slot(source_dev, take)
        if which == 0:
            own_out[...] = acc[...]
        else:
            far_out[...] = acc[...].astype(far_out.dtype)


def couple(exc, counts, couplings, own, left, right, far_a, far_b, sib):
    rows, cols = own.shape
    full = lambda *shape: pl.BlockSpec(shape, lambda i, *_: (0,) * len(shape))
    arrays = (couplings, own, left, right, far_a, far_b, sib)
    return pl.pallas_call(
        couple_kernel,
        grid_spec=pltpu.PrefetchScalarGridSpec(
            num_scalar_prefetch=2,
            grid=(1,),
            in_specs=[full(*a.shape) for a in arrays],
            out_specs=[full(rows, cols), full(rows, cols)],
            scratch_shapes=[pltpu.VMEM((rows, cols), jnp.float32)],
        ),
        out_shape=[
            jax.ShapeDtypeStruct((rows, cols), jnp.float32),
            jax.ShapeDtypeStruct((rows, cols), jnp.bfloat16),
        ],
        cost_estimate=pl.CostEstimate(
            flops=2 * 16 * AB * AB * cols, bytes_accessed=12 * rows * cols * 2, transcendentals=0
        ),
        compiler_params=pltpu.CompilerParams(vmem_limit_bytes=32 << 20),
    )(exc, counts, *arrays)


def exchange(own, exc, counts, couplings):
    left = lax.ppermute(own, "alpha", to_x(1))
    right = lax.ppermute(own, "alpha", to_x(-1))
    far_a = lax.ppermute(left[:AB], "alpha", to_x(1))
    far_b = lax.ppermute(right[AB:], "alpha", to_x(-1))
    mine = jnp.concatenate([own, right, far_a, far_b, left], axis=0)
    sib = lax.ppermute(mine, "alpha", SWAP_CORE)
    near, far = couple(exc, counts, couplings, own, left, right, far_a, far_b, sib)
    back = lax.ppermute(far, "alpha", SWAP_Y)
    return (near + back.astype(jnp.float32)).astype(jnp.bfloat16)


def per_device(coefficients, couplings, exc_list, counts, beta_tiles):
    exc = exc_list.reshape(exc_list.shape[0], -1)
    total = None
    start = 0
    for width in CHUNKS:
        span = slice(start, start + width)
        start += width
        moving = exchange(coefficients[:, span], exc, counts, couplings)
        for offset in range(STOPS):
            if offset:
                moving = next_beta(moving)
            part = jnp.dot(moving, beta_tiles[offset, span], preferred_element_type=jnp.float32)
            total = part if total is None else total + part
    return total


def solution(mesh):
    placed = (P("alpha", "beta"), P(), P(), P(), P(None, None, "beta"))
    return jax.shard_map(
        per_device, mesh=mesh, in_specs=placed, out_specs=P("alpha", "beta"), check_vma=False
    )
```

```python
import functools

import jax
import jax.numpy as jnp
from jax import lax
from jax.experimental import pallas as pl
from jax.experimental.pallas import tpu as pltpu
from jax.sharding import PartitionSpec as P

AB = 256
ABLK = 2
STOPS = 4
NX = 4
NZ = 8
ROWS = ABLK * AB
EARLY = 128
CHUNKS = (128, 256, 256, 256)
ROW_TILE = 128

VMEM = pl.BlockSpec(memory_space=pltpu.VMEM)
SMEM = pl.BlockSpec(memory_space=pltpu.SMEM)


def device_of(y, x, core):
    return (y * NX + x) * 2 + core


def alpha_route(move):
    route = []
    for y in range(2):
        for x in range(NX):
            for core in range(2):
                to = move(y, x, core)
                route.append((device_of(y, x, core), device_of(*to)))
    return route


def to_x(step):
    return alpha_route(lambda y, x, core: (y, (x + step) % NX, core))


SWAP_CORE = alpha_route(lambda y, x, core: (y, x, 1 - core))
SWAP_Y = alpha_route(lambda y, x, core: (1 - y, x, core))
RING = [(i, (i + 1) % (2 * NZ)) for i in range(2 * NZ)]
COLUMN = [(y * NZ + z, y * NZ + (z + 1) % NZ) for y in range(2) for z in range(NZ)]
CROSS = [(NZ - 1, 2 * NZ - 1), (2 * NZ - 1, NZ - 1)]


def after(value, *earlier):
    return lax.optimization_barrier((value, *earlier))[0]


def slot_codes(exc_list, counts):
    me = lax.axis_index("alpha")
    y = me // (2 * NX)
    mates = 2 * NX
    exc = lax.dynamic_slice_in_dim(exc_list, y * mates, mates, 0)
    live = lax.dynamic_slice_in_dim(counts, y * mates, mates, 0) == 1
    codes = []
    for target in (me, (me + mates) % (2 * mates)):
        entry = lax.dynamic_index_in_dim(exc, target, 1, keepdims=False)
        used = lax.dynamic_index_in_dim(live, target, 1, keepdims=False)
        source = entry[:, 0] - (y * mates + jnp.arange(mates, dtype=jnp.int32)) * ABLK
        goal = entry[:, 1] - target * ABLK
        codes.append(jnp.where(used, (entry[:, 2] * 2 + goal) * 2 + source, -1))
    return jnp.concatenate(codes)


def couple_kernel(which, codes, coup, mine, sib, out, *scratch):
    me = lax.axis_index("alpha")
    x, core = (me // 2) % NX, me % 2
    total = scratch[0] if scratch else out
    total[...] = jnp.zeros_like(total)
    for stack, side in ((mine, core), (sib, 1 - core)):

        @pl.loop(0, NX)
        def _(step):
            code = codes[which * 2 * NX + lax.rem(x + step, NX) * 2 + side]

            @pl.when(code >= 0)
            def _():
                kind, goal, source = code // 4, (code // 2) % 2, code % 2
                rows = pl.ds(pl.multiple_of(goal * AB, AB), AB)
                block = stack[pl.ds(pl.multiple_of(step * ROWS + source * AB, AB), AB), :]
                total[rows, :] += jnp.dot(coup[kind], block, preferred_element_type=jnp.float32)

    if scratch:
        out[...] = total[...].astype(out.dtype)


def couple(which, codes, couplings, mine, sib):
    cols = mine.shape[1]
    kind = jnp.float32 if which == 0 else jnp.bfloat16
    return pl.pallas_call(
        functools.partial(couple_kernel, which),
        in_specs=[SMEM] + [VMEM] * 3,
        out_specs=VMEM,
        scratch_shapes=[] if which == 0 else [pltpu.VMEM((ROWS, cols), jnp.float32)],
        out_shape=jax.ShapeDtypeStruct((ROWS, cols), kind),
        cost_estimate=pl.CostEstimate(
            flops=16 * AB * AB * cols, bytes_accessed=10 * ROWS * cols * 2, transcendentals=0
        ),
        compiler_params=pltpu.CompilerParams(vmem_limit_bytes=8 << 20),
    )(codes, couplings, mine, sib)


def band_kernel(places, first, *refs):
    n = len(places)
    blocks, tiles = refs[:n], refs[n]
    before, out = (None, refs[n + 1]) if first else refs[n + 1 :]

    @pl.loop(0, ROWS, step=ROW_TILE)
    def _(row):
        rows = pl.ds(pl.multiple_of(row, ROW_TILE), ROW_TILE)
        for k, (shift, start, width, lane) in enumerate(places):
            part = jnp.dot(
                blocks[k][rows, lane : lane + width],
                tiles[shift, start : start + width, :],
                preferred_element_type=jnp.float32,
            )
            if k > 0:
                out[rows, :] += part
            elif first:
                out[rows, :] = part
            else:
                out[rows, :] = before[rows, :] + part


def band(total, tiles, blocks, places):
    first = total is None
    cols = tiles.shape[2]
    flops = sum(2 * ROWS * p[2] * cols for p in places)
    arrays = list(blocks) + [tiles] + ([] if first else [total])
    return pl.pallas_call(
        functools.partial(band_kernel, tuple(places), first),
        in_specs=[VMEM] * len(arrays),
        out_specs=VMEM,
        out_shape=jax.ShapeDtypeStruct((ROWS, cols), jnp.float32),
        input_output_aliases={} if first else {len(arrays) - 1: 0},
        cost_estimate=pl.CostEstimate(flops=flops, bytes_accessed=4 << 20, transcendentals=0),
        compiler_params=pltpu.CompilerParams(vmem_limit_bytes=8 << 20),
    )(*arrays)


def per_device(coefficients, couplings, exc_list, counts, beta_tiles):
    corner = lax.axis_index("beta") % NZ == NZ - 1
    codes = slot_codes(exc_list, counts)

    def spread(own):
        return [own] + [lax.ppermute(own, "alpha", to_x(s)) for s in (-1, 2, 1)]

    def ring(block):
        crossed = lax.ppermute(block, "beta", CROSS)
        one = lax.ppermute(jnp.where(corner, crossed, block), "beta", COLUMN)
        two = lax.ppermute(one, "beta", RING)
        return [block, one, two, lax.ppermute(two, "beta", RING)]

    early = [coefficients[:, :EARLY]]
    for _ in range(STOPS - 1):
        early.append(lax.ppermute(early[-1], "beta", RING))
    starts = [EARLY + sum(CHUNKS[:k]) for k in range(len(CHUNKS))]
    owns = [coefficients[:, s : s + w] for s, w in zip(starts, CHUNKS)] + [jnp.concatenate(early, axis=1)]

    count = len(owns)
    spreads = [spread(owns[0]), spread(owns[1])] + [None] * (count - 2)
    outs = []
    total = None
    for k in range(count):
        mine = jnp.concatenate(spreads[k], axis=0)
        sib = lax.ppermute(mine, "alpha", SWAP_CORE)
        if k > 0:
            sib = after(sib, outs[k - 1][0])
        away = couple(1, codes, couplings, mine, sib)
        back = lax.ppermute(away, "alpha", SWAP_Y)
        if k + 2 < count:
            spreads[k + 2] = spread(after(owns[k + 2], away))
        near = couple(0, codes, couplings, mine, sib)
        done = (near + back.astype(jnp.float32)).astype(jnp.bfloat16)
        outs.append(ring(done) if k < count - 1 else [done])
    for k, width in enumerate(CHUNKS):
        places = [(d, starts[k], width, 0) for d in range(STOPS)]
        if k < len(CHUNKS) - 1:
            total = band(total, beta_tiles, outs[k], places)
        else:
            total = band(total, beta_tiles, outs[k][:-1], places[:-1])
            last = outs[k][-1:], places[-1:]
    total = band(total, beta_tiles, outs[-1] * STOPS, [(d, 0, EARLY, d * EARLY) for d in range(STOPS)])
    return band(total, beta_tiles, *last)


def solution(mesh):
    placed = (P("alpha", "beta"), P(), P(), P(), P(None, None, "beta"))
    return jax.shard_map(
        per_device, mesh=mesh, in_specs=placed, out_specs=P("alpha", "beta"), check_vma=False
    )
```

```python
import functools

import jax
import jax.numpy as jnp
from jax import lax
from jax.experimental import pallas as pl
from jax.experimental.pallas import tpu as pltpu
from jax.sharding import PartitionSpec as P

AB = 256
ABLK = 2
STOPS = 4
NX = 4
NZ = 8
ROWS = ABLK * AB
EARLY = 384
PARTS = 2
COLUMN_TILE = 256

COST = pl.CostEstimate(flops=1 << 20, bytes_accessed=1 << 12, transcendentals=0)
VMEM = pl.BlockSpec(memory_space=pltpu.VMEM)
SMEM = pl.BlockSpec(memory_space=pltpu.SMEM)


def device_of(y, x, core):
    return (y * NX + x) * 2 + core


def alpha_route(move):
    route = []
    for y in range(2):
        for x in range(NX):
            for core in range(2):
                to = move(y, x, core)
                route.append((device_of(y, x, core), device_of(*to)))
    return route


def to_x(step):
    return alpha_route(lambda y, x, core: (y, (x + step) % NX, core))


SWAP_CORE = alpha_route(lambda y, x, core: (y, x, 1 - core))
SWAP_Y = alpha_route(lambda y, x, core: (1 - y, x, core))
RING = [(i, (i + 1) % (2 * NZ)) for i in range(2 * NZ)]


def after(value, *earlier):
    return lax.optimization_barrier((value, *earlier))[0]


def slot_codes(exc_list, counts):
    me = lax.axis_index("alpha")
    y = me // (2 * NX)
    mates = 2 * NX
    exc = lax.dynamic_slice_in_dim(exc_list, y * mates, mates, 0)
    live = lax.dynamic_slice_in_dim(counts, y * mates, mates, 0) == 1
    codes = []
    for target in (me, (me + mates) % (2 * mates)):
        entry = lax.dynamic_index_in_dim(exc, target, 1, keepdims=False)
        used = lax.dynamic_index_in_dim(live, target, 1, keepdims=False)
        source = entry[:, 0] - (y * mates + jnp.arange(mates, dtype=jnp.int32)) * ABLK
        goal = entry[:, 1] - target * ABLK
        codes.append(jnp.where(used, (entry[:, 2] * 2 + goal) * 2 + source, -1))
    return jnp.concatenate(codes)


def couple_kernel(codes, coup, mine, sib, near, away, acc):
    me = lax.axis_index("alpha")
    x, core = (me // 2) % NX, me % 2
    near[...] = jnp.zeros_like(near)
    acc[...] = jnp.zeros_like(acc)
    for which, total in enumerate((near, acc)):
        for stack, side in ((mine, core), (sib, 1 - core)):

            @pl.loop(0, NX)
            def _(step):
                code = codes[which * 2 * NX + lax.rem(x + step, NX) * 2 + side]

                @pl.when(code >= 0)
                def _():
                    kind, goal, source = code // 4, (code // 2) % 2, code % 2
                    rows = pl.ds(pl.multiple_of(goal * AB, AB), AB)
                    block = stack[pl.ds(pl.multiple_of(step * ROWS + source * AB, AB), AB), :]
                    total[rows, :] += jnp.dot(coup[kind], block, preferred_element_type=jnp.float32)

    away[...] = acc[...].astype(away.dtype)


def couple(codes, couplings, mine, sib):
    cols = mine.shape[1]
    return pl.pallas_call(
        couple_kernel,
        in_specs=[SMEM] + [VMEM] * 3,
        out_specs=[VMEM, VMEM],
        scratch_shapes=[pltpu.VMEM((ROWS, cols), jnp.float32)],
        out_shape=[
            jax.ShapeDtypeStruct((ROWS, cols), jnp.float32),
            jax.ShapeDtypeStruct((ROWS, cols), jnp.bfloat16),
        ],
        cost_estimate=COST,
        compiler_params=pltpu.CompilerParams(vmem_limit_bytes=12 << 20),
    )(codes, couplings, mine, sib)


def stack_kernel(*refs):
    out = refs[-1]
    row = 0
    for ref in refs[:-1]:
        out[row : row + ref.shape[0], :] = ref[...]
        row += ref.shape[0]


def stack(blocks):
    rows, cols = sum(b.shape[0] for b in blocks), blocks[0].shape[1]
    return pl.pallas_call(
        stack_kernel,
        in_specs=[VMEM] * len(blocks),
        out_specs=VMEM,
        out_shape=jax.ShapeDtypeStruct((rows, cols), jnp.bfloat16),
        cost_estimate=COST,
        compiler_params=pltpu.CompilerParams(vmem_limit_bytes=4 << 20),
    )(*blocks)


def band_kernel(pieces, first, *refs):
    n = len(pieces)
    blocks, tiles = refs[:n], refs[n]
    before, out = (None, refs[n + 1]) if first else refs[n + 1 :]

    @pl.loop(0, tiles.shape[2], step=COLUMN_TILE)
    def _(column):
        span = pl.ds(pl.multiple_of(column, COLUMN_TILE), COLUMN_TILE)
        left = jnp.concatenate([block[...] for block in blocks], axis=1)
        right = jnp.concatenate([tiles[d, s : s + w, span] for d, s, w in pieces], axis=0)
        part = jnp.dot(left, right, preferred_element_type=jnp.float32)
        if not first:
            part = before[:, span] + part
        out[:, span] = part.astype(out.dtype)


def band(total, tiles, blocks, pieces, kind=jnp.float32):
    first = total is None
    arrays = list(blocks) + [tiles] + ([] if first else [total])
    return pl.pallas_call(
        functools.partial(band_kernel, tuple(pieces), first),
        in_specs=[VMEM] * len(arrays),
        out_specs=VMEM,
        out_shape=jax.ShapeDtypeStruct((ROWS, tiles.shape[2]), kind),
        input_output_aliases={} if first else {len(arrays) - 1: 0},
        cost_estimate=COST,
        compiler_params=pltpu.CompilerParams(vmem_limit_bytes=12 << 20),
    )(*arrays)


def tie(*values):
    return list(lax.optimization_barrier(values))


def per_device(coefficients, couplings, exc_list, counts, beta_tiles):
    codes = slot_codes(exc_list, counts)

    def spread(own):
        left = lax.ppermute(own, "alpha", to_x(1))
        right = lax.ppermute(own, "alpha", to_x(-1))
        far = [
            lax.ppermute(left[:AB], "alpha", to_x(1)),
            lax.ppermute(right[AB:], "alpha", to_x(-1)),
        ]
        return [own, right, *far, left]

    def hop(block):
        return lax.ppermute(block, "beta", RING)

    cols = coefficients.shape[1]
    early = [coefficients[:, :EARLY]]
    for _ in range(STOPS - 1):
        early.append(hop(early[-1]))
    parts = spread(coefficients[:, EARLY:])
    *parts, early[3] = tie(*parts, early[3])
    mine = stack(parts)
    sib = lax.ppermute(mine, "alpha", SWAP_CORE)
    mixed = band(None, beta_tiles, early, [(d, 0, EARLY) for d in range(STOPS)], jnp.bfloat16)
    sib, mixed = tie(sib, mixed)
    near, away = couple(codes, couplings, mine, sib)
    back = lax.ppermute(away, "alpha", SWAP_Y)
    moved = [(near + back.astype(jnp.float32)).astype(jnp.bfloat16)]

    parts = spread(mixed)
    moved.append(hop(moved[0]))
    moved.append(hop(moved[1]))
    *parts, moved[2] = tie(*parts, moved[2])
    moved.append(hop(moved[2]))
    half = cols // PARTS
    mines = [stack([p[:, k * half : (k + 1) * half] for p in parts]) for k in range(PARTS)]
    sibs = [lax.ppermute(m, "alpha", SWAP_CORE) for m in mines]
    nears, backs = [], []
    for k in range(PARTS):
        if k:
            sibs[k], away = tie(sibs[k], away)
            backs[k - 1] = lax.ppermute(away, "alpha", SWAP_Y)
        near, away = couple(codes, couplings, mines[k], sibs[k])
        nears.append(near)
        backs.append(lax.ppermute(away, "alpha", SWAP_Y))
    width = cols - EARLY
    total = band(None, beta_tiles, moved[:3], [(d, EARLY, width) for d in range(3)])
    moved[3], total = tie(moved[3], total)
    total = total + jnp.dot(moved[3], beta_tiles[3, EARLY:], preferred_element_type=jnp.float32)
    near, back = jnp.concatenate(nears, axis=1), jnp.concatenate(backs, axis=1)
    return total + (near + back.astype(jnp.float32))


def solution(mesh):
    placed = (P("alpha", "beta"), P(), P(), P(), P(None, None, "beta"))
    return jax.shard_map(
        per_device, mesh=mesh, in_specs=placed, out_specs=P("alpha", "beta"), check_vma=False
    )
```

```python
import functools

import jax
import jax.numpy as jnp
from jax import lax
from jax.experimental import pallas as pl
from jax.experimental.pallas import tpu as pltpu
from jax.sharding import PartitionSpec as P

AB = 256
ABLK = 2
STOPS = 4
NX = 4
NZ = 8
ROWS = ABLK * AB
EARLY = 512
PARTS = 2
COLUMN_TILE = 256

COST = pl.CostEstimate(flops=1 << 20, bytes_accessed=1 << 12, transcendentals=0)
VMEM = pl.BlockSpec(memory_space=pltpu.VMEM)
SMEM = pl.BlockSpec(memory_space=pltpu.SMEM)


def device_of(y, x, core):
    return (y * NX + x) * 2 + core


def alpha_route(move):
    route = []
    for y in range(2):
        for x in range(NX):
            for core in range(2):
                to = move(y, x, core)
                route.append((device_of(y, x, core), device_of(*to)))
    return route


def to_x(step):
    return alpha_route(lambda y, x, core: (y, (x + step) % NX, core))


SWAP_CORE = alpha_route(lambda y, x, core: (y, x, 1 - core))
SWAP_Y = alpha_route(lambda y, x, core: (1 - y, x, core))
RING = [(i, (i + 1) % (2 * NZ)) for i in range(2 * NZ)]


def after(value, *earlier):
    return lax.optimization_barrier((value, *earlier))[0]


def slot_codes(exc_list, counts):
    me = lax.axis_index("alpha")
    y = me // (2 * NX)
    mates = 2 * NX
    exc = lax.dynamic_slice_in_dim(exc_list, y * mates, mates, 0)
    live = lax.dynamic_slice_in_dim(counts, y * mates, mates, 0) == 1
    codes = []
    for target in (me, (me + mates) % (2 * mates)):
        entry = lax.dynamic_index_in_dim(exc, target, 1, keepdims=False)
        used = lax.dynamic_index_in_dim(live, target, 1, keepdims=False)
        source = entry[:, 0] - (y * mates + jnp.arange(mates, dtype=jnp.int32)) * ABLK
        goal = entry[:, 1] - target * ABLK
        codes.append(jnp.where(used, (entry[:, 2] * 2 + goal) * 2 + source, -1))
    return jnp.concatenate(codes)


def couple_kernel(codes, coup, mine, sib, near, away, acc):
    me = lax.axis_index("alpha")
    x, core = (me // 2) % NX, me % 2
    near[...] = jnp.zeros_like(near)
    acc[...] = jnp.zeros_like(acc)
    for which, total in enumerate((near, acc)):
        for stack, side in ((mine, core), (sib, 1 - core)):

            @pl.loop(0, NX)
            def _(step):
                code = codes[which * 2 * NX + lax.rem(x + step, NX) * 2 + side]

                @pl.when(code >= 0)
                def _():
                    kind, goal, source = code // 4, (code // 2) % 2, code % 2
                    rows = pl.ds(pl.multiple_of(goal * AB, AB), AB)
                    taken = pl.ds(pl.multiple_of(step * ROWS + source * AB, AB), AB)
                    matrix = coup[kind]
                    for column in range(0, stack.shape[1], COLUMN_TILE):
                        span = slice(column, min(column + COLUMN_TILE, stack.shape[1]))
                        total[rows, span] += jnp.dot(
                            matrix, stack[taken, span], preferred_element_type=jnp.float32
                        )

    away[...] = acc[...].astype(away.dtype)


def couple(codes, couplings, mine, sib):
    cols = mine.shape[1]
    return pl.pallas_call(
        couple_kernel,
        in_specs=[SMEM] + [VMEM] * 3,
        out_specs=[VMEM, VMEM],
        scratch_shapes=[pltpu.VMEM((ROWS, cols), jnp.float32)],
        out_shape=[
            jax.ShapeDtypeStruct((ROWS, cols), jnp.float32),
            jax.ShapeDtypeStruct((ROWS, cols), jnp.bfloat16),
        ],
        cost_estimate=COST,
        compiler_params=pltpu.CompilerParams(vmem_limit_bytes=12 << 20),
    )(codes, couplings, mine, sib)


def stack_kernel(*refs):
    out = refs[-1]
    row = 0
    for ref in refs[:-1]:
        out[row : row + ref.shape[0], :] = ref[...]
        row += ref.shape[0]


def stack(blocks):
    rows, cols = sum(b.shape[0] for b in blocks), blocks[0].shape[1]
    return pl.pallas_call(
        stack_kernel,
        in_specs=[VMEM] * len(blocks),
        out_specs=VMEM,
        out_shape=jax.ShapeDtypeStruct((rows, cols), jnp.bfloat16),
        cost_estimate=COST,
        compiler_params=pltpu.CompilerParams(vmem_limit_bytes=4 << 20),
    )(*blocks)


def product(block, tile):
    return jnp.dot(block, tile, preferred_element_type=jnp.float32)


def tie(*values):
    return list(lax.optimization_barrier(values))


def per_device(coefficients, couplings, exc_list, counts, beta_tiles):
    codes = slot_codes(exc_list, counts)

    def spread(own):
        left = lax.ppermute(own, "alpha", to_x(1))
        right = lax.ppermute(own, "alpha", to_x(-1))
        far = [
            lax.ppermute(left[:AB], "alpha", to_x(1)),
            lax.ppermute(right[AB:], "alpha", to_x(-1)),
        ]
        return [own, right, *far, left]

    def hop(block):
        return lax.ppermute(block, "beta", RING)

    cols = coefficients.shape[1]
    early = coefficients[:, :EARLY]
    arrived = hop(early)
    mixed = product(early, beta_tiles[0, :EARLY])
    parts = spread(coefficients[:, EARLY:])
    for d in range(1, STOPS - 1):
        arrived, mixed = tie(arrived, mixed)
        early, arrived = arrived, hop(arrived)
        if d < STOPS - 2:
            mixed = mixed + product(early, beta_tiles[d, :EARLY])
    *parts, mixed, early = tie(*parts, mixed, early)
    mine = stack(parts)
    sib = lax.ppermute(mine, "alpha", SWAP_CORE)
    near, away = couple(codes, couplings, mine, sib)
    early, mixed, _ = tie(early, mixed, away)
    mixed = mixed + product(early, beta_tiles[STOPS - 2, :EARLY])
    arrived, mixed = tie(arrived, mixed)
    mixed = (mixed + product(arrived, beta_tiles[STOPS - 1, :EARLY])).astype(jnp.bfloat16)
    back = lax.ppermute(away, "alpha", SWAP_Y)
    moved = [(near + back.astype(jnp.float32)).astype(jnp.bfloat16)]

    parts = spread(mixed)
    moved.append(hop(moved[0]))
    total = product(moved[0], beta_tiles[0, EARLY:])
    moved[1], parts[1], parts[4], total = tie(moved[1], parts[1], parts[4], total)
    moved.append(hop(moved[1]))
    *parts, _ = tie(*parts, moved[2])
    half = coefficients.shape[1] // PARTS
    mines = [stack([p[:, k * half : (k + 1) * half] for p in parts]) for k in range(PARTS)]
    sibs = [lax.ppermute(m, "alpha", SWAP_CORE) for m in mines]
    nears, backs = [], []
    for k in range(PARTS):
        if k:
            sibs[k] = after(sibs[k], away)
        near, away = couple(codes, couplings, mines[k], sibs[k])
        nears.append(near)
        backs.append(lax.ppermute(away, "alpha", SWAP_Y))
    total = total + product(moved[1], beta_tiles[1, EARLY:])
    moved.append(hop(moved[2]))
    total = total + product(moved[2], beta_tiles[2, EARLY:])
    moved[3], total = tie(moved[3], total)
    total = total + product(moved[3], beta_tiles[3, EARLY:])
    near, back = jnp.concatenate(nears, axis=1), jnp.concatenate(backs, axis=1)
    return total + (near + back.astype(jnp.float32))


def solution(mesh):
    placed = (P("alpha", "beta"), P(), P(), P(), P(None, None, "beta"))
    return jax.shard_map(
        per_device, mesh=mesh, in_specs=placed, out_specs=P("alpha", "beta"), check_vma=False
    )
```

```python
import functools

import jax
import jax.numpy as jnp
from jax import lax
from jax.experimental import pallas as pl
from jax.experimental.pallas import tpu as pltpu
from jax.sharding import PartitionSpec as P

AB = 256
ABLK = 2
STOPS = 4
NX = 4
NZ = 8
ROWS = ABLK * AB
EARLY = 512
PARTS = 2
COLUMN_TILE = 256

COST = pl.CostEstimate(flops=1 << 20, bytes_accessed=1 << 12, transcendentals=0)
VMEM = pl.BlockSpec(memory_space=pltpu.VMEM)
SMEM = pl.BlockSpec(memory_space=pltpu.SMEM)


def device_of(y, x, core):
    return (y * NX + x) * 2 + core


def alpha_route(move):
    route = []
    for y in range(2):
        for x in range(NX):
            for core in range(2):
                to = move(y, x, core)
                route.append((device_of(y, x, core), device_of(*to)))
    return route


def to_x(step):
    return alpha_route(lambda y, x, core: (y, (x + step) % NX, core))


SWAP_CORE = alpha_route(lambda y, x, core: (y, x, 1 - core))
SWAP_Y = alpha_route(lambda y, x, core: (1 - y, x, core))
RING = [(i, (i + 1) % (2 * NZ)) for i in range(2 * NZ)]


def after(value, *earlier):
    return lax.optimization_barrier((value, *earlier))[0]


def slot_codes(exc_list, counts):
    me = lax.axis_index("alpha")
    y = me // (2 * NX)
    mates = 2 * NX
    exc = lax.dynamic_slice_in_dim(exc_list, y * mates, mates, 0)
    live = lax.dynamic_slice_in_dim(counts, y * mates, mates, 0) == 1
    codes = []
    for target in (me, (me + mates) % (2 * mates)):
        entry = lax.dynamic_index_in_dim(exc, target, 1, keepdims=False)
        used = lax.dynamic_index_in_dim(live, target, 1, keepdims=False)
        source = entry[:, 0] - (y * mates + jnp.arange(mates, dtype=jnp.int32)) * ABLK
        goal = entry[:, 1] - target * ABLK
        codes.append(jnp.where(used, (entry[:, 2] * 2 + goal) * 2 + source, -1))
    return jnp.concatenate(codes)


def couple_kernel(codes, coup, mine, sib, near, away, acc):
    me = lax.axis_index("alpha")
    x, core = (me // 2) % NX, me % 2
    near[...] = jnp.zeros_like(near)
    acc[...] = jnp.zeros_like(acc)
    for which, total in enumerate((near, acc)):
        for stack, side in ((mine, core), (sib, 1 - core)):

            @pl.loop(0, NX)
            def _(step):
                code = codes[which * 2 * NX + lax.rem(x + step, NX) * 2 + side]

                @pl.when(code >= 0)
                def _():
                    kind, goal, source = code // 4, (code // 2) % 2, code % 2
                    rows = pl.ds(pl.multiple_of(goal * AB, AB), AB)
                    taken = pl.ds(pl.multiple_of(step * ROWS + source * AB, AB), AB)
                    matrix = coup[kind]
                    for column in range(0, stack.shape[1], COLUMN_TILE):
                        span = slice(column, min(column + COLUMN_TILE, stack.shape[1]))
                        total[rows, span] += jnp.dot(
                            matrix, stack[taken, span], preferred_element_type=jnp.float32
                        )

    away[...] = acc[...].astype(away.dtype)


def couple(codes, couplings, mine, sib):
    cols = mine.shape[1]
    return pl.pallas_call(
        couple_kernel,
        in_specs=[SMEM] + [VMEM] * 3,
        out_specs=[VMEM, VMEM],
        scratch_shapes=[pltpu.VMEM((ROWS, cols), jnp.float32)],
        out_shape=[
            jax.ShapeDtypeStruct((ROWS, cols), jnp.float32),
            jax.ShapeDtypeStruct((ROWS, cols), jnp.bfloat16),
        ],
        cost_estimate=COST,
        compiler_params=pltpu.CompilerParams(vmem_limit_bytes=12 << 20),
    )(codes, couplings, mine, sib)


def stack_kernel(*refs):
    out = refs[-1]
    row = 0
    for ref in refs[:-1]:
        out[row : row + ref.shape[0], :] = ref[...]
        row += ref.shape[0]


def stack(blocks):
    rows, cols = sum(b.shape[0] for b in blocks), blocks[0].shape[1]
    return pl.pallas_call(
        stack_kernel,
        in_specs=[VMEM] * len(blocks),
        out_specs=VMEM,
        out_shape=jax.ShapeDtypeStruct((rows, cols), jnp.bfloat16),
        cost_estimate=COST,
        compiler_params=pltpu.CompilerParams(vmem_limit_bytes=4 << 20),
    )(*blocks)


def product(block, tile):
    return jnp.dot(block, tile, preferred_element_type=jnp.float32)


def tie(*values):
    return list(lax.optimization_barrier(values))


def per_device(coefficients, couplings, exc_list, counts, beta_tiles):
    codes = slot_codes(exc_list, counts)

    def spread(own):
        left = lax.ppermute(own, "alpha", to_x(1))
        right = lax.ppermute(own, "alpha", to_x(-1))
        far = [
            lax.ppermute(left[:AB], "alpha", to_x(1)),
            lax.ppermute(right[AB:], "alpha", to_x(-1)),
        ]
        return [own, right, *far, left]

    def hop(block):
        return lax.ppermute(block, "beta", RING)

    cols = coefficients.shape[1]
    early = coefficients[:, :EARLY]
    arrived = [hop(early[:, : EARLY // 2]), hop(early[:, EARLY // 2 :])]
    mixed = product(early, beta_tiles[0, :EARLY])
    parts = spread(coefficients[:, EARLY:])
    for d in range(1, STOPS - 1):
        arrived[0], mixed = tie(arrived[0], mixed)
        early, arrived = arrived, [hop(block) for block in arrived]
        if d < STOPS - 2:
            mixed = mixed + product(jnp.concatenate(early, axis=1), beta_tiles[d, :EARLY])
    *parts, mixed, early[0], early[1] = tie(*parts, mixed, *early)
    mine = stack(parts)
    sib = lax.ppermute(mine, "alpha", SWAP_CORE)
    near, away = couple(codes, couplings, mine, sib)
    *early, mixed, _ = tie(*early, mixed, away)
    mixed = mixed + product(jnp.concatenate(early, axis=1), beta_tiles[STOPS - 2, :EARLY])
    *arrived, mixed = tie(*arrived, mixed)
    arrived = jnp.concatenate(arrived, axis=1)
    mixed = (mixed + product(arrived, beta_tiles[STOPS - 1, :EARLY])).astype(jnp.bfloat16)
    back = lax.ppermute(away, "alpha", SWAP_Y)
    moved = [(near + back.astype(jnp.float32)).astype(jnp.bfloat16)]

    parts = spread(mixed)
    moved.append(hop(moved[0]))
    total = product(moved[0], beta_tiles[0, EARLY:])
    moved[1], parts[1], parts[4], total = tie(moved[1], parts[1], parts[4], total)
    moved.append(hop(moved[1]))
    *parts, _ = tie(*parts, moved[2])
    half = coefficients.shape[1] // PARTS
    mines = [stack([p[:, k * half : (k + 1) * half] for p in parts]) for k in range(PARTS)]
    sibs = [lax.ppermute(m, "alpha", SWAP_CORE) for m in mines]
    nears, backs = [], []
    for k in range(PARTS):
        if k:
            sibs[k] = after(sibs[k], away)
        near, away = couple(codes, couplings, mines[k], sibs[k])
        nears.append(near)
        backs.append(lax.ppermute(away, "alpha", SWAP_Y))
    total = total + product(moved[1], beta_tiles[1, EARLY:])
    moved.append(hop(moved[2]))
    total = total + product(moved[2], beta_tiles[2, EARLY:])
    moved[3], total = tie(moved[3], total)
    total = total + product(moved[3], beta_tiles[3, EARLY:])
    near, back = jnp.concatenate(nears, axis=1), jnp.concatenate(backs, axis=1)
    return total + (near + back.astype(jnp.float32))


def solution(mesh):
    placed = (P("alpha", "beta"), P(), P(), P(), P(None, None, "beta"))
    return jax.shard_map(
        per_device, mesh=mesh, in_specs=placed, out_specs=P("alpha", "beta"), check_vma=False
    )
```

```python
import functools

import jax
import jax.numpy as jnp
from jax import lax
from jax.experimental import pallas as pl
from jax.experimental.pallas import tpu as pltpu
from jax.sharding import PartitionSpec as P

AB = 256
ABLK = 2
STOPS = 4
NX = 4
NZ = 8
ROWS = ABLK * AB
EARLY = 512
PARTS = 1
COLUMN_TILE = 256

COST = pl.CostEstimate(flops=1 << 20, bytes_accessed=1 << 12, transcendentals=0)
VMEM = pl.BlockSpec(memory_space=pltpu.VMEM)
SMEM = pl.BlockSpec(memory_space=pltpu.SMEM)


def device_of(y, x, core):
    return (y * NX + x) * 2 + core


def alpha_route(move):
    route = []
    for y in range(2):
        for x in range(NX):
            for core in range(2):
                to = move(y, x, core)
                route.append((device_of(y, x, core), device_of(*to)))
    return route


def to_x(step):
    return alpha_route(lambda y, x, core: (y, (x + step) % NX, core))


SWAP_CORE = alpha_route(lambda y, x, core: (y, x, 1 - core))
SWAP_Y = alpha_route(lambda y, x, core: (1 - y, x, core))
RING = [(i, (i + 1) % (2 * NZ)) for i in range(2 * NZ)]


def after(value, *earlier):
    return lax.optimization_barrier((value, *earlier))[0]


def slot_codes(exc_list, counts):
    me = lax.axis_index("alpha")
    y = me // (2 * NX)
    mates = 2 * NX
    exc = lax.dynamic_slice_in_dim(exc_list, y * mates, mates, 0)
    live = lax.dynamic_slice_in_dim(counts, y * mates, mates, 0) == 1
    codes = []
    for target in (me, (me + mates) % (2 * mates)):
        entry = lax.dynamic_index_in_dim(exc, target, 1, keepdims=False)
        used = lax.dynamic_index_in_dim(live, target, 1, keepdims=False)
        source = entry[:, 0] - (y * mates + jnp.arange(mates, dtype=jnp.int32)) * ABLK
        goal = entry[:, 1] - target * ABLK
        codes.append(jnp.where(used, (entry[:, 2] * 2 + goal) * 2 + source, -1))
    return jnp.concatenate(codes)


def couple_kernel(codes, coup, mine, sib, near, away, acc):
    me = lax.axis_index("alpha")
    x, core = (me // 2) % NX, me % 2
    near[...] = jnp.zeros_like(near)
    acc[...] = jnp.zeros_like(acc)
    for which, total in enumerate((near, acc)):
        for stack, side in ((mine, core), (sib, 1 - core)):

            @pl.loop(0, NX)
            def _(step):
                code = codes[which * 2 * NX + lax.rem(x + step, NX) * 2 + side]

                @pl.when(code >= 0)
                def _():
                    kind, goal, source = code // 4, (code // 2) % 2, code % 2
                    rows = pl.ds(pl.multiple_of(goal * AB, AB), AB)
                    taken = pl.ds(pl.multiple_of(step * ROWS + source * AB, AB), AB)
                    matrix = coup[kind]
                    for column in range(0, stack.shape[1], COLUMN_TILE):
                        span = slice(column, min(column + COLUMN_TILE, stack.shape[1]))
                        total[rows, span] += jnp.dot(
                            matrix, stack[taken, span], preferred_element_type=jnp.float32
                        )

    away[...] = acc[...].astype(away.dtype)


def couple(codes, couplings, mine, sib):
    cols = mine.shape[1]
    return pl.pallas_call(
        couple_kernel,
        in_specs=[SMEM] + [VMEM] * 3,
        out_specs=[VMEM, VMEM],
        scratch_shapes=[pltpu.VMEM((ROWS, cols), jnp.float32)],
        out_shape=[
            jax.ShapeDtypeStruct((ROWS, cols), jnp.float32),
            jax.ShapeDtypeStruct((ROWS, cols), jnp.bfloat16),
        ],
        cost_estimate=COST,
        compiler_params=pltpu.CompilerParams(vmem_limit_bytes=12 << 20),
    )(codes, couplings, mine, sib)


def stack_kernel(*refs):
    out = refs[-1]
    row = 0
    for ref in refs[:-1]:
        out[row : row + ref.shape[0], :] = ref[...]
        row += ref.shape[0]


def stack(blocks):
    rows, cols = sum(b.shape[0] for b in blocks), blocks[0].shape[1]
    return pl.pallas_call(
        stack_kernel,
        in_specs=[VMEM] * len(blocks),
        out_specs=VMEM,
        out_shape=jax.ShapeDtypeStruct((rows, cols), jnp.bfloat16),
        cost_estimate=COST,
        compiler_params=pltpu.CompilerParams(vmem_limit_bytes=4 << 20),
    )(*blocks)


def product(block, tile):
    return jnp.dot(block, tile, preferred_element_type=jnp.float32)


def tie(*values):
    return list(lax.optimization_barrier(values))


def per_device(coefficients, couplings, exc_list, counts, beta_tiles):
    codes = slot_codes(exc_list, counts)

    def spread(own):
        left = lax.ppermute(own, "alpha", to_x(1))
        right = lax.ppermute(own, "alpha", to_x(-1))
        far = [
            lax.ppermute(left[:AB], "alpha", to_x(1)),
            lax.ppermute(right[AB:], "alpha", to_x(-1)),
        ]
        return [own, right, *far, left]

    def hop(block):
        return lax.ppermute(block, "beta", RING)

    cols = coefficients.shape[1]
    early = coefficients[:, :EARLY]
    arrived = [hop(early[:, : EARLY // 2]), hop(early[:, EARLY // 2 :])]
    mixed = product(early, beta_tiles[0, :EARLY])
    parts = spread(coefficients[:, EARLY:])
    for d in range(1, STOPS - 1):
        arrived[0], mixed = tie(arrived[0], mixed)
        early, arrived = arrived, [hop(block) for block in arrived]
        if d < STOPS - 2:
            mixed = mixed + product(jnp.concatenate(early, axis=1), beta_tiles[d, :EARLY])
    *parts, mixed, early[0], early[1] = tie(*parts, mixed, *early)
    mine = stack(parts)
    sib = lax.ppermute(mine, "alpha", SWAP_CORE)
    near, away = couple(codes, couplings, mine, sib)
    *early, mixed, _ = tie(*early, mixed, away)
    mixed = mixed + product(jnp.concatenate(early, axis=1), beta_tiles[STOPS - 2, :EARLY])
    *arrived, mixed = tie(*arrived, mixed)
    arrived = jnp.concatenate(arrived, axis=1)
    mixed = (mixed + product(arrived, beta_tiles[STOPS - 1, :EARLY])).astype(jnp.bfloat16)
    back = lax.ppermute(away, "alpha", SWAP_Y)
    moved = [(near + back.astype(jnp.float32)).astype(jnp.bfloat16)]

    parts = spread(mixed)
    moved.append(hop(moved[0]))
    total = product(moved[0], beta_tiles[0, EARLY:])
    moved[1], parts[1], parts[4], total = tie(moved[1], parts[1], parts[4], total)
    moved.append(hop(moved[1]))
    *parts, _ = tie(*parts, moved[2])
    half = coefficients.shape[1] // PARTS
    mines = [stack([p[:, k * half : (k + 1) * half] for p in parts]) for k in range(PARTS)]
    sibs = [lax.ppermute(m, "alpha", SWAP_CORE) for m in mines]
    nears, backs = [], []
    for k in range(PARTS):
        if k:
            sibs[k] = after(sibs[k], away)
        near, away = couple(codes, couplings, mines[k], sibs[k])
        nears.append(near)
        backs.append(lax.ppermute(away, "alpha", SWAP_Y))
    total = total + product(moved[1], beta_tiles[1, EARLY:])
    moved.append(hop(moved[2]))
    total = total + product(moved[2], beta_tiles[2, EARLY:])
    moved[3], total = tie(moved[3], total)
    total = total + product(moved[3], beta_tiles[3, EARLY:])
    near, back = jnp.concatenate(nears, axis=1), jnp.concatenate(backs, axis=1)
    return total + (near + back.astype(jnp.float32))


def solution(mesh):
    placed = (P("alpha", "beta"), P(), P(), P(), P(None, None, "beta"))
    return jax.shard_map(
        per_device, mesh=mesh, in_specs=placed, out_specs=P("alpha", "beta"), check_vma=False
    )
```
